256 devices in a mesh: seq: 16 (over x, y), fsdp: 16 (over z, core).
Axes of the slice: x: 4, y: 4, z: 8, core: 2. Of those that a mesh axis runs over, the one named last changes fastest.
Arguments:
- patches: bfloat16 [16, 8704, 1176], P('fsdp', 'seq'), may hold values from -6 to 6
- send_slot: int32 [16, 272], P('fsdp', 'seq'), may hold values from 0 to 271, as said below
- segments: int32 [16, 272], P('fsdp'), may hold values from 0 to 33, never falling along the last dimension, each value on 1 to 24 neighbouring positions
- stem_weight: bfloat16 [3584, 1176], P('fsdp'), may hold values from -0.1875 to 0.1875
- norm_gain: bfloat16 [3584], P('fsdp'), may hold values from 0.099609375 to 1.8984375
- conv_kernel: bfloat16 [5, 3584], P(None, 'fsdp'), may hold values from -3 to 3
- cotangent: bfloat16 [16, 8704, 3584], P('fsdp', 'seq'), may hold values from -6 to 6
Outputs:
- features: bfloat16 [16, 8704, 3584], P('fsdp', 'seq')
- grad_patches: bfloat16 [16, 8704, 1176], P('fsdp', 'seq')
- grad_weight: bfloat16 [3584, 1176], P('fsdp')
- grad_channels: float32 [6, 3584], P(None, 'fsdp')
The draws below stay inside these ranges and needn't reach their ends.
Inputs may be any that keep to these rules, and one draw needn't show every extreme that they name: `send_slot`: each row is a permutation of the packed slots. At most 2 frame slots of one device go to one device's packed slots, and every device sends exactly 2 to some device; within a row the number that device s sends to device (s + o) modulo the seq axis size depends on o alone. `segments`: ids never fall along a row; a clip holds 1 to 24 slots, one exactly 24.
All inputs are finite; a program needn't handle non-finite values.
Results may differ from the reference program's by a relative error of at most 0.0056.
Values may be sent and summed in bfloat16 or wider, within the bound.
A program may use at most 192 MiB of HBM per device.

```python
import math
import jax
import jax.numpy as jnp
import numpy as np
from jax import lax

D = 3584
P_SIZE = 1176
SP = 32
SLOTS_DEV = 17
CLIP_MOST = 24
TOK_DEV = 544
SEQ_SLOTS = 272
SEQ_ROWS = 8704
CLIPS = 34
ALL_TOKENS = 139264
N_SEQ = 16
N_FSDP = 16


def owner_plan(key):
    device_total = N_SEQ
    slot_total = SLOTS_DEV
    capacity = 2 * SLOTS_DEV // N_SEQ
    subkeys = jax.random.split(key, 4)
    copies = jnp.arange(device_total * capacity, dtype=jnp.int32)
    offsets = copies // capacity
    forced = jax.random.randint(subkeys[0], (), 0, device_total, dtype=jnp.int32)
    shuffled = jax.random.permutation(subkeys[1], device_total * capacity).astype(jnp.int32)
    scores = jnp.where(offsets == forced, copies % capacity - capacity, shuffled)
    chosen = offsets[jnp.argsort(scores)[:slot_total]]
    row_keys = jax.random.split(subkeys[2], device_total)
    slot_offsets = jax.vmap(lambda row_key: chosen[jax.random.permutation(row_key, slot_total)])(row_keys)
    owner_index = (jnp.arange(device_total, dtype=jnp.int32)[:, None] + slot_offsets) % device_total
    flat_owner = owner_index.reshape(-1)
    onehot = (flat_owner[:, None] == jnp.arange(device_total, dtype=jnp.int32)[None, :]).astype(jnp.int32)
    arrival = jnp.sum((jnp.cumsum(onehot, axis=0) - onehot) * onehot, axis=1)
    order_keys = jax.random.split(subkeys[3], device_total)
    orders = jax.vmap(lambda row_key: jax.random.permutation(row_key, slot_total))(order_keys).astype(jnp.int32)
    return (flat_owner * slot_total + orders[flat_owner, arrival]).astype(jnp.int32)


def draw_send_slot(key, part):
    base_key = jax.random.fold_in(key, 11)
    return jax.vmap(owner_plan)(jax.random.split(base_key, N_FSDP))


def strengthened(values, key, source, target, blocks, factor):
    owner, partner = [(jnp.arange(values.shape[axis_at]) // (values.shape[axis_at] // blocks)).reshape([-1 if axis == axis_at else 1 for axis in range(values.ndim)]) for axis_at in (source, target)]
    chosen = jax.random.permutation(key, blocks)[partner]
    strong = (owner == chosen) | (owner == (partner + blocks // 2) % blocks)
    return jnp.where(strong, factor * values, values)


def levels(own_key, shape, cuts, low, top_value):
    gain = 1.0
    for axis_at, shards_of in cuts:
        draws = jax.random.uniform(jax.random.fold_in(jax.random.fold_in(own_key, 6), axis_at), (shards_of,), jnp.float32, low / len(cuts), top_value / len(cuts))
        gain = gain * jnp.repeat(jnp.exp(draws), shape[axis_at] // shards_of).reshape((-1,) + (1,) * (len(shape) - 1 - axis_at))
    return gain


def split_up(number_of, total, reach, lean):
    weights = [(1 << 20) // math.isqrt(standing ** lean) + 1 for standing in range(2, number_of + 1)]
    surplus, counts = total - reach - (number_of - 1), [1] * (number_of - 1)
    while surplus > 0:
        free = [i for i in range(number_of - 1) if counts[i] < reach]
        mass, left = sum([weights[i] for i in free]), surplus
        for i in free:
            more = min(reach - counts[i], max(1, left * weights[i] // mass), surplus)
            counts[i] = counts[i] + more
            surplus = surplus - more
    return np.array([reach] + counts)


def ragged(rng, number_of, total, reach, skew):
    if number_of == 2:
        one = jax.random.randint(rng, (), max(1, total - reach), min(reach, total - 1) + 1)
        return jnp.stack([one, total - one])
    sizes = jnp.asarray(split_up(number_of, total, reach, skew), jnp.int32)
    pairs = (number_of - 1) // 2
    giver, sink = sizes[1:1 + 2 * pairs:2], sizes[2:2 + 2 * pairs:2]
    margin = jnp.minimum(giver - 1, reach - sink)
    moved = jax.random.randint(jax.random.fold_in(rng, 1), (pairs,), 0, 1 << 20) % (margin + 1)
    sizes = sizes.at[1:1 + 2 * pairs:2].set(giver - moved).at[2:2 + 2 * pairs:2].set(sink + moved)
    return sizes[jax.random.permutation(jax.random.fold_in(rng, 2), number_of)]


def bell_draw(own_key, shape, deviation, most, cuts=(), kind=jnp.bfloat16):
    values = jax.random.normal(own_key, shape, jnp.float32) * deviation
    if len(cuts) > 0:
        values = levels(own_key, shape, cuts, -0.22, 0.18) * values
    return jnp.clip(values, min=-most, max=most).astype(kind)


def heavy_noise(key, dims, deviation, bound, cuts, heavy, kind=jnp.bfloat16):
    values = deviation * jax.random.normal(key, dims, jnp.float32)
    if cuts:
        values = values * levels(key, dims, cuts, -0.22, 0.18)
    return jnp.clip(strengthened(values, jax.random.fold_in(key, 3), *heavy), -bound, bound).astype(kind)


def setup_inputs(seed: int = 0) -> dict:
    arg_keys = jax.random.split(jax.random.key(seed), 8)
    return {
        "patches": bell_draw(arg_keys[0], (N_FSDP, SEQ_ROWS, P_SIZE), 1.0, 6.0, ((0, 16), (1, 16))),
        "send_slot": draw_send_slot(jax.random.fold_in(arg_keys[7], 71), 0),
        "segments": jax.vmap(lambda own: jnp.searchsorted(jnp.cumsum(ragged(own, CLIPS, SEQ_SLOTS, CLIP_MOST, 1)), jnp.arange(SEQ_SLOTS), side="right"))(jax.random.split(arg_keys[2], N_FSDP)).reshape((N_FSDP, SEQ_SLOTS)).astype(jnp.int32),
        "stem_weight": bell_draw(arg_keys[3], (D, P_SIZE), P_SIZE ** -0.5, 0.1875, ((0, 16),)),
        "norm_gain": jnp.clip(1.0 + 0.18 * jax.random.normal(arg_keys[4], (D,), jnp.float32), 0.099609375, 1.8984375).astype(jnp.bfloat16),
        "conv_kernel": bell_draw(arg_keys[5], (5, D), 0.5, 3.0, ((1, 16),)),
        "cotangent": heavy_noise(arg_keys[6], (N_FSDP, SEQ_ROWS, D), 1.0, 6.0, ((0, 16), (1, 16)), (0, 2, 16, 2.0)),
    }


EPSILON = 1e-06

def slot_mask(segment_row, centre):
    slot_total = segment_row.shape[0]
    safe_centre = jnp.clip(centre, 0, slot_total - 1)
    columns = []
    for offset in range(5):
        neighbour = centre + (offset - 2)
        inside = (neighbour >= 0) & (neighbour < slot_total) & (centre >= 0) & (centre < slot_total)
        same_clip = segment_row[jnp.clip(neighbour, 0, slot_total - 1)] == segment_row[safe_centre]
        columns.append((inside & same_clip).astype(jnp.float32))
    return jnp.stack(columns, axis=1)

def temporal_mix(padded, clip_mask, kernel, slot_total):
    kernel_wide = kernel.astype(jnp.float32)
    result = padded[0:slot_total].astype(jnp.float32) * (clip_mask[:, 0][:, None, None] * kernel_wide[0][None, None, :])
    for offset in range(1, 5):
        addend = padded[offset:offset + slot_total].astype(jnp.float32) * (clip_mask[:, offset][:, None, None] * kernel_wide[offset][None, None, :])
        result = result + addend
    return result

def temporal_back(slope_padded, mask_padded, kernel, slot_total):
    kernel_wide = kernel.astype(jnp.float32)
    result = jnp.zeros((slot_total,) + slope_padded.shape[1:], jnp.float32)
    for offset in range(5):
        first_row = 4 - offset
        weights_row = mask_padded[first_row:first_row + slot_total, offset][:, None, None] * kernel_wide[offset][None, None, :]
        result = result + slope_padded[first_row:first_row + slot_total].astype(jnp.float32) * weights_row
    return result

def kernel_terms(slope_blocks, padded, clip_mask, slot_total):
    stacked = []
    for offset in range(5):
        product = lax.optimization_barrier(jnp.sum(slope_blocks.astype(jnp.float32) * padded[offset:offset + slot_total].astype(jnp.float32), axis=1))
        stacked.append(product * clip_mask[:, offset][:, None])
    return jnp.stack(stacked, axis=1)

def reference(patches, send_slot, segments, stem_weight, norm_gain, conv_kernel, cotangent):
    gain_wide = norm_gain.astype(jnp.float32)
    centre = jnp.arange(SEQ_SLOTS, dtype=jnp.int32)
    extended = jnp.arange(-2, SEQ_SLOTS + 2, dtype=jnp.int32)
    pad_slots = ((2, 2), (0, 0), (0, 0))

    def one_group(totals, inputs):
        weight_total, chan_total = totals
        patch_rows, destination, segment_row, upstream = inputs
        frames = patch_rows.reshape(SEQ_SLOTS, SP, P_SIZE)
        packed = jnp.zeros_like(frames).at[destination].set(frames).reshape(SEQ_ROWS, P_SIZE)
        stem_out = jnp.dot(packed, stem_weight.T, preferred_element_type=jnp.float32)
        inv_rms = lax.rsqrt(lax.optimization_barrier(jnp.mean(stem_out * stem_out, axis=1, keepdims=True)) + EPSILON)
        unit_rows = stem_out * inv_rms
        normed = (unit_rows * gain_wide).astype(jnp.bfloat16)
        clip_mask = slot_mask(segment_row, centre)
        padded = jnp.pad(normed.reshape(SEQ_SLOTS, SP, D), pad_slots)
        mixed_rows = temporal_mix(padded, clip_mask, conv_kernel, SEQ_SLOTS).reshape(SEQ_ROWS, D)
        features = (stem_out + jax.nn.silu(mixed_rows)).astype(jnp.bfloat16)
        gate_value = jax.nn.sigmoid(mixed_rows)
        upstream_wide = upstream.astype(jnp.float32)
        slope_low = (upstream_wide * gate_value * (1.0 + mixed_rows * (1.0 - gate_value))).astype(jnp.bfloat16)
        slope_blocks = slope_low.reshape(SEQ_SLOTS, SP, D)
        mask_padded = slot_mask(segment_row, extended)
        d_normed = temporal_back(jnp.pad(slope_blocks, pad_slots), mask_padded, conv_kernel, SEQ_SLOTS).reshape(SEQ_ROWS, D)
        gated = d_normed * gain_wide
        d_stem = upstream_wide + inv_rms * (gated - unit_rows * lax.optimization_barrier(jnp.mean(gated * unit_rows, axis=1, keepdims=True)))
        d_stem_low = d_stem.astype(jnp.bfloat16)
        grad_rows = jnp.dot(d_stem_low, stem_weight, preferred_element_type=jnp.float32).astype(jnp.bfloat16)
        gain_part = lax.optimization_barrier(jnp.sum((d_normed * unit_rows).reshape(N_SEQ, TOK_DEV, D), axis=1))
        kernel_part = lax.optimization_barrier(jnp.sum(kernel_terms(slope_blocks, padded, clip_mask, SEQ_SLOTS).reshape(N_SEQ, SLOTS_DEV, 5, D), axis=1))
        chan_part = jnp.concatenate([gain_part[:, None, :], kernel_part], axis=1)
        chan_total = chan_total + lax.optimization_barrier(jnp.sum(chan_part, axis=0))

        def device_term(running, pieces):
            grad_piece, input_piece = pieces
            weight_part = lax.dot_general(grad_piece, input_piece, (((0,), (0,)), ((), ())), preferred_element_type=jnp.float32)
            return (running + weight_part, None)
        weight_total, unused = lax.scan(device_term, weight_total, (d_stem_low.reshape(N_SEQ, TOK_DEV, D), packed.reshape(N_SEQ, TOK_DEV, P_SIZE)))
        return ((weight_total, chan_total), (features, grad_rows))
    zeros_weight = jnp.zeros((D, P_SIZE), jnp.float32)
    zeros_chan = jnp.zeros((6, D), jnp.float32)
    totals, outputs = lax.scan(one_group, (zeros_weight, zeros_chan), (patches, send_slot, segments, cotangent))
    grad_scale = 1.0 / ALL_TOKENS ** 0.5
    grad_weight = (totals[0] * grad_scale).astype(jnp.bfloat16)
    grad_channels = totals[1] * grad_scale
    return (outputs[0], outputs[1], grad_weight, grad_channels)
```

```python
import math

import jax
import jax.numpy as jnp
from jax import lax
from jax.sharding import PartitionSpec as P

EPSILON = 1e-06


def pl_ceil(total, step):
    return -(-total // step)


def extended_2(cells, sides, width):
    for axis, dim in sides:
        count = lax.axis_size(axis)
        ends = count - 1
        head = lax.slice_in_dim(cells, 0, width, axis=dim)
        tail = lax.slice_in_dim(cells, cells.shape[dim] - width, cells.shape[dim], axis=dim)
        cells = jnp.concatenate(
            [
                lax.ppermute(tail, axis, [(i, (i + 1) % count) for i in range(ends)]),
                cells,
                lax.ppermute(head, axis, [((i + 1) % count, i) for i in range(ends)]),
            ],
            axis=dim,
        )
    return cells


def slot_mask(segment_row, centre):
    slot_total = segment_row.shape[0]
    safe_centre = jnp.clip(centre, 0, slot_total - 1)
    columns = []
    for offset in range(5):
        neighbour = centre + (offset - 2)
        inside = (neighbour >= 0) & (neighbour < slot_total) & (centre >= 0) & (centre < slot_total)
        same_clip = segment_row[jnp.clip(neighbour, 0, slot_total - 1)] == segment_row[safe_centre]
        columns.append((inside & same_clip).astype(jnp.float32))
    return jnp.stack(columns, axis=1)


def temporal_mix(padded, clip_mask, kernel, slot_total):
    kernel_wide = kernel.astype(jnp.float32)
    result = padded[0:slot_total].astype(jnp.float32) * (
        clip_mask[:, 0][:, None, None] * kernel_wide[0][None, None, :]
    )
    for offset in range(1, 5):
        addend = padded[offset : offset + slot_total].astype(jnp.float32) * (
            clip_mask[:, offset][:, None, None] * kernel_wide[offset][None, None, :]
        )
        result = result + addend
    return result


def temporal_back(slope_padded, mask_padded, kernel, slot_total):
    kernel_wide = kernel.astype(jnp.float32)
    result = jnp.zeros((slot_total,) + slope_padded.shape[1:], jnp.float32)
    for offset in range(5):
        first_row = 4 - offset
        weights_row = (
            mask_padded[first_row : first_row + slot_total, offset][:, None, None]
            * kernel_wide[offset][None, None, :]
        )
        result = (
            result
            + slope_padded[first_row : first_row + slot_total].astype(jnp.float32) * weights_row
        )
    return result


def kernel_sums(slope_blocks, padded, clip_mask, slot_total):
    stacked = []
    for offset in range(5):
        product = jnp.sum(
            slope_blocks.astype(jnp.float32)
            * padded[offset : offset + slot_total].astype(jnp.float32),
            axis=1,
        )
        stacked.append(jnp.sum(product * clip_mask[:, offset][:, None], axis=0))
    return jnp.stack(stacked, axis=0)


def rim_rows(values, margin):
    return extended_2(values, (("seq", 0),), margin)


def shards(patches, send_slot, segments, stem_weight, norm_gain, conv_kernel, cotangent):
    seq_size = lax.axis_size("seq")
    fsdp_size = lax.axis_size("fsdp")
    seq_index = lax.axis_index("seq")
    slot_count = send_slot.shape[1]
    tokens = patches.shape[1]
    slot_rows = tokens // slot_count
    pixel_width = patches.shape[2]
    capacity = 2 * slot_count // seq_size
    destination = send_slot[0]
    owner_index = destination // slot_count
    same_owner = owner_index[:, None] == owner_index[None, :]
    earlier = destination[None, :] < destination[:, None]
    ranking = jnp.sum((same_owner & earlier).astype(jnp.int32), axis=1)
    buffer_row = owner_index * capacity + ranking
    frames = patches[0].reshape(slot_count, slot_rows, pixel_width)
    outbox = (
        jnp.zeros((seq_size * capacity, slot_rows, pixel_width), jnp.bfloat16)
        .at[buffer_row]
        .set(frames)
    )
    position = (
        jnp.full((seq_size * capacity,), -1.0, jnp.float32)
        .at[buffer_row]
        .set((destination % slot_count).astype(jnp.float32))
        .astype(jnp.bfloat16)
    )
    incoming, arrived = (
        lax.all_to_all(outbox, "seq", split_axis=0, concat_axis=0, tiled=True),
        lax.all_to_all(position, "seq", split_axis=0, concat_axis=0, tiled=True),
    )
    arrived_float = arrived.astype(jnp.float32)
    target = jnp.where(arrived_float >= 0.0, arrived_float, float(slot_count)).astype(jnp.int32)
    packed = (
        jnp.zeros((slot_count + 1, slot_rows, pixel_width), jnp.bfloat16)
        .at[target]
        .set(incoming)[:slot_count]
        .reshape(tokens, pixel_width)
    )
    extras = jnp.concatenate([norm_gain[:, None], conv_kernel.T], axis=1)
    shard_ext = jnp.concatenate([stem_weight, extras], axis=1)
    gathered = lax.all_gather(shard_ext, "fsdp", axis=0, tiled=True)
    weight_full = gathered[:, :pixel_width]
    channel_low = gathered[:, pixel_width:].T
    gain_low = channel_low[0]
    kernel_full = channel_low[1:]
    gain_wide = gain_low.astype(jnp.float32)
    channels = weight_full.shape[0]
    stem_out = lax.dot_general(
        packed, weight_full, (((1,), (1,)), ((), ())), preferred_element_type=jnp.float32
    )
    inv_rms = lax.rsqrt(jnp.mean(stem_out * stem_out, axis=1, keepdims=True) + EPSILON)
    unit_rows = stem_out * inv_rms
    normed = (unit_rows * gain_wide).astype(jnp.bfloat16)
    segment_row = segments[0]
    centre = seq_index * slot_count + jnp.arange(slot_count, dtype=jnp.int32)
    extended = seq_index * slot_count + jnp.arange(-2, slot_count + 2, dtype=jnp.int32)
    clip_mask = slot_mask(segment_row, centre)
    mask_padded = slot_mask(segment_row, extended)
    padded = rim_rows(normed, 2 * slot_rows).reshape(slot_count + 4, slot_rows, channels)
    mixed_rows = temporal_mix(padded, clip_mask, kernel_full, slot_count).reshape(tokens, channels)
    features = (stem_out + jax.nn.silu(mixed_rows)).astype(jnp.bfloat16)
    upstream_wide = cotangent[0].astype(jnp.float32)
    gate_value = jax.nn.sigmoid(mixed_rows)
    slope_low = (upstream_wide * gate_value * (1.0 + mixed_rows * (1.0 - gate_value))).astype(
        jnp.bfloat16
    )
    slope_padded = rim_rows(slope_low, 2 * slot_rows).reshape(slot_count + 4, slot_rows, channels)
    d_normed = temporal_back(slope_padded, mask_padded, kernel_full, slot_count).reshape(
        tokens, channels
    )
    gated = d_normed * gain_wide
    d_stem = upstream_wide + inv_rms * (
        gated - unit_rows * jnp.mean(gated * unit_rows, axis=1, keepdims=True)
    )
    d_stem_low = d_stem.astype(jnp.bfloat16)
    grad_rows = jnp.dot(d_stem_low, weight_full, preferred_element_type=jnp.float32).astype(
        jnp.bfloat16
    )
    gain_part = jnp.sum(d_normed * unit_rows, axis=0)
    slope_blocks = slope_padded[2 : 2 + slot_count]
    kernel_part = kernel_sums(slope_blocks, padded, clip_mask, slot_count)
    chan_terms = jnp.concatenate([gain_part[None, :], kernel_part], axis=0).T
    weight_block = lax.dot_general(
        d_stem_low,
        jnp.pad(packed, ((0, 0), (0, 6))),
        (((0,), (0,)), ((), ())),
        preferred_element_type=jnp.float32,
    )
    total_block = weight_block + jnp.pad(chan_terms, ((0, 0), (pixel_width, 0)))
    panel = channels // fsdp_size
    panel_padded = 16 * seq_size * pl_ceil(panel, 16 * seq_size)
    stacked = jnp.pad(
        total_block.reshape(fsdp_size, panel, pixel_width + 6),
        ((0, 0), (0, panel_padded - panel), (0, 0)),
    ).reshape(fsdp_size * panel_padded, pixel_width + 6)
    piece = lax.psum_scatter(stacked, ("fsdp", "seq"), scatter_dimension=0, tiled=True)
    grad_scale = 1.0 / math.sqrt(tokens * seq_size * fsdp_size)
    summed = lax.all_gather(piece * grad_scale, "seq", axis=0, tiled=True)[:panel]
    grad_weight = summed[:, :pixel_width].astype(jnp.bfloat16)
    grad_channels = summed[:, pixel_width:].T
    return (features[None], grad_rows[None], grad_weight, grad_channels)


def solution(mesh):
    in_specs = (
        P("fsdp", "seq", None),
        P("fsdp", "seq"),
        P("fsdp", None),
        P("fsdp", None),
        P("fsdp"),
        P(None, "fsdp"),
        P("fsdp", "seq", None),
    )
    out_specs = (P("fsdp", "seq", None), P("fsdp", "seq", None), P("fsdp", None), P(None, "fsdp"))
    return jax.shard_map(shards, mesh=mesh, in_specs=in_specs, out_specs=out_specs, check_vma=False)
```

```python
import math

import jax
import jax.numpy as jnp
from jax import lax
from jax.experimental import pallas as pl
from jax.experimental.pallas import tpu as pltpu
from jax.sharding import PartitionSpec as P

EPSILON = 1e-06


def weight_body(d_ref, packed_ref, chan_ref, out_ref):
    acc = lax.dot_general(
        d_ref[...], packed_ref[...], (((0,), (0,)), ((), ())), preferred_element_type=jnp.float32
    )
    edge = acc.shape[1] - chan_ref.shape[1]
    out_ref[...] = acc
    out_ref[:, edge:] = acc[:, edge:] + chan_ref[...]


def weight_grad(d_stem_low, packed_wide, chan_edge):
    tokens, channels = d_stem_low.shape
    width = packed_wide.shape[1]
    block = 896
    return pl.pallas_call(
        weight_body,
        grid=(channels // block,),
        in_specs=[
            pl.BlockSpec((tokens, block), lambda i: (0, i)),
            pl.BlockSpec((tokens, width), lambda i: (0, 0)),
            pl.BlockSpec((block, chan_edge.shape[1]), lambda i: (i, 0)),
        ],
        out_specs=pl.BlockSpec((block, width), lambda i: (i, 0)),
        out_shape=jax.ShapeDtypeStruct((channels, width), jnp.float32),
    )(d_stem_low, packed_wide, chan_edge)


def back_body(
    mask_ref, mask_wide_ref, slope_ref, normed_ref, stem_ref, inv_ref, gain_ref, kern_ref,
    gated_ref, row_ref, chan_ref,
):
    rows = 32
    slot_total = stem_ref.shape[0] // rows
    cols = stem_ref.shape[1]

    @pl.when(pl.program_id(0) == 0)
    def _():
        row_ref[...] = jnp.zeros_like(row_ref)

    gain = gain_ref[...]
    taps = [kern_ref[k : k + 1, :] for k in range(5)]
    gain_acc = jnp.zeros((8, cols), jnp.float32)
    kern_acc = [jnp.zeros((8, cols), jnp.float32) for _ in range(5)]

    def fold(v):
        return v[0:8] + v[8:16] + v[16:24] + v[24:32]

    for g in range(slot_total):
        here = slice(g * rows, (g + 1) * rows)
        d = jnp.zeros((rows, cols), jnp.float32)
        for k in range(5):
            p = g + 4 - k
            d = d + slope_ref[p * rows : (p + 1) * rows, :].astype(jnp.float32) * (
                mask_wide_ref[p, k] * taps[k]
            )
        unit = stem_ref[here, :] * inv_ref[here, :]
        gated = d * gain
        gated_ref[here, :] = gated
        row_ref[here, :] += jnp.sum(gated * unit, axis=1, keepdims=True)
        gain_acc = gain_acc + fold(d * unit)
        own = slope_ref[(g + 2) * rows : (g + 3) * rows, :].astype(jnp.float32)
        for k in range(5):
            q = g + k
            prod = own * normed_ref[q * rows : (q + 1) * rows, :].astype(jnp.float32)
            kern_acc[k] = kern_acc[k] + mask_ref[g, k] * fold(prod)
    chan_ref[0:1, :] = jnp.sum(gain_acc, axis=0, keepdims=True)
    for k in range(5):
        chan_ref[k + 1 : k + 2, :] = jnp.sum(kern_acc[k], axis=0, keepdims=True)
    chan_ref[6:8, :] = jnp.zeros((2, cols), jnp.float32)


def back_pass(clip_mask, mask_padded, slope_padded, padded, stem_out, inv_rms, gain, kernel):
    tokens, channels = stem_out.shape
    wide = slope_padded.shape[0]
    block = 512
    whole = pl.BlockSpec(memory_space=pltpu.SMEM)

    def columns(rows):
        return pl.BlockSpec((rows, block), lambda i: (0, i))

    row_spec = pl.BlockSpec((tokens, 1), lambda i: (0, 0))
    return pl.pallas_call(
        back_body,
        grid=(channels // block,),
        in_specs=[
            whole, whole, columns(wide), columns(wide), columns(tokens), row_spec, columns(1),
            columns(5),
        ],
        out_specs=[columns(tokens), row_spec, columns(8)],
        out_shape=[
            jax.ShapeDtypeStruct((tokens, channels), jnp.float32),
            jax.ShapeDtypeStruct((tokens, 1), jnp.float32),
            jax.ShapeDtypeStruct((8, channels), jnp.float32),
        ],
    )(clip_mask, mask_padded, slope_padded, padded, stem_out, inv_rms, gain, kernel)


def extended_2(cells, sides, width):
    for axis, dim in sides:
        count = lax.axis_size(axis)
        ends = count - 1
        head = lax.slice_in_dim(cells, 0, width, axis=dim)
        tail = lax.slice_in_dim(cells, cells.shape[dim] - width, cells.shape[dim], axis=dim)
        cells = jnp.concatenate(
            [
                lax.ppermute(tail, axis, [(i, (i + 1) % count) for i in range(ends)]),
                cells,
                lax.ppermute(head, axis, [((i + 1) % count, i) for i in range(ends)]),
            ],
            axis=dim,
        )
    return cells


def slot_mask(segment_row, centre):
    slot_total = segment_row.shape[0]
    safe_centre = jnp.clip(centre, 0, slot_total - 1)
    columns = []
    for offset in range(5):
        neighbour = centre + (offset - 2)
        inside = (neighbour >= 0) & (neighbour < slot_total) & (centre >= 0) & (centre < slot_total)
        same_clip = segment_row[jnp.clip(neighbour, 0, slot_total - 1)] == segment_row[safe_centre]
        columns.append((inside & same_clip).astype(jnp.float32))
    return jnp.stack(columns, axis=1)


def temporal_mix(padded, clip_mask, kernel, slot_total):
    kernel_wide = kernel.astype(jnp.float32)
    result = padded[0:slot_total].astype(jnp.float32) * (
        clip_mask[:, 0][:, None, None] * kernel_wide[0][None, None, :]
    )
    for offset in range(1, 5):
        addend = padded[offset : offset + slot_total].astype(jnp.float32) * (
            clip_mask[:, offset][:, None, None] * kernel_wide[offset][None, None, :]
        )
        result = result + addend
    return result


def rim_rows(values, margin):
    return extended_2(values, (("seq", 0),), margin)


def shards(patches, send_slot, segments, stem_weight, norm_gain, conv_kernel, cotangent):
    seq_size = lax.axis_size("seq")
    fsdp_size = lax.axis_size("fsdp")
    seq_index = lax.axis_index("seq")
    slot_count = send_slot.shape[1]
    tokens = patches.shape[1]
    slot_rows = tokens // slot_count
    pixel_width = patches.shape[2]
    capacity = 2 * slot_count // seq_size
    destination = send_slot[0]
    owner_index = destination // slot_count
    same_owner = owner_index[:, None] == owner_index[None, :]
    earlier = destination[None, :] < destination[:, None]
    ranking = jnp.sum((same_owner & earlier).astype(jnp.int32), axis=1)
    buffer_row = owner_index * capacity + ranking
    frames = patches[0].reshape(slot_count, slot_rows, pixel_width)
    outbox = (
        jnp.zeros((seq_size * capacity, slot_rows, pixel_width), jnp.bfloat16)
        .at[buffer_row]
        .set(frames)
    )
    position = (
        jnp.full((seq_size * capacity,), -1.0, jnp.float32)
        .at[buffer_row]
        .set((destination % slot_count).astype(jnp.float32))
        .astype(jnp.bfloat16)
    )
    incoming, arrived = (
        lax.all_to_all(outbox, "seq", split_axis=0, concat_axis=0, tiled=True),
        lax.all_to_all(position, "seq", split_axis=0, concat_axis=0, tiled=True),
    )
    arrived_float = arrived.astype(jnp.float32)
    target = jnp.where(arrived_float >= 0.0, arrived_float, float(slot_count)).astype(jnp.int32)
    packed = (
        jnp.zeros((slot_count + 1, slot_rows, pixel_width), jnp.bfloat16)
        .at[target]
        .set(incoming)[:slot_count]
        .reshape(tokens, pixel_width)
    )
    extras = jnp.concatenate([norm_gain[:, None], conv_kernel.T], axis=1)
    shard_ext = jnp.concatenate([stem_weight, extras], axis=1)
    gathered = lax.all_gather(shard_ext, "fsdp", axis=0, tiled=True)
    weight_full = gathered[:, :pixel_width]
    channel_low = gathered[:, pixel_width:].T
    gain_low = channel_low[0]
    kernel_full = channel_low[1:]
    gain_wide = gain_low.astype(jnp.float32)
    channels = weight_full.shape[0]
    stem_out = lax.dot_general(
        packed, weight_full, (((1,), (1,)), ((), ())), preferred_element_type=jnp.float32
    )
    inv_rms = lax.rsqrt(jnp.mean(stem_out * stem_out, axis=1, keepdims=True) + EPSILON)
    unit_rows = stem_out * inv_rms
    normed = (unit_rows * gain_wide).astype(jnp.bfloat16)
    segment_row = segments[0]
    centre = seq_index * slot_count + jnp.arange(slot_count, dtype=jnp.int32)
    extended = seq_index * slot_count + jnp.arange(-2, slot_count + 2, dtype=jnp.int32)
    clip_mask = slot_mask(segment_row, centre)
    mask_padded = slot_mask(segment_row, extended)
    padded_rows = rim_rows(normed, 2 * slot_rows)
    padded = padded_rows.reshape(slot_count + 4, slot_rows, channels)
    mixed_rows = temporal_mix(padded, clip_mask, kernel_full, slot_count).reshape(tokens, channels)
    features = (stem_out + jax.nn.silu(mixed_rows)).astype(jnp.bfloat16)
    upstream_wide = cotangent[0].astype(jnp.float32)
    gate_value = jax.nn.sigmoid(mixed_rows)
    slope_low = (upstream_wide * gate_value * (1.0 + mixed_rows * (1.0 - gate_value))).astype(
        jnp.bfloat16
    )
    slope_rows = rim_rows(slope_low, 2 * slot_rows)
    gated, row_sum, chan_rows = back_pass(
        clip_mask,
        mask_padded,
        slope_rows,
        padded_rows,
        stem_out,
        inv_rms,
        gain_wide[None, :],
        kernel_full.astype(jnp.float32),
    )
    d_stem = upstream_wide + inv_rms * (
        gated - unit_rows * (row_sum / channels)
    )
    d_stem_low = d_stem.astype(jnp.bfloat16)
    grad_rows = jnp.dot(d_stem_low, weight_full, preferred_element_type=jnp.float32).astype(
        jnp.bfloat16
    )
    chan_edge = jnp.pad(chan_rows[:6].T, ((0, 0), (24, 0)))
    total_block = weight_grad(d_stem_low, jnp.pad(packed, ((0, 0), (0, 6))), chan_edge)
    shard = lax.psum_scatter(total_block, "fsdp", scatter_dimension=0, tiled=True)
    panel = channels // fsdp_size
    part_rows = 16
    width = pixel_width + 6
    parts = jnp.pad(shard.astype(jnp.bfloat16), ((0, part_rows * seq_size - panel), (0, 0)))
    spread = lax.all_to_all(parts, "seq", split_axis=0, concat_axis=0, tiled=True)
    grad_scale = 1.0 / math.sqrt(tokens * seq_size * fsdp_size)
    piece = jnp.sum(spread.reshape(seq_size, part_rows, width).astype(jnp.float32), axis=0)
    piece = (piece * grad_scale).astype(jnp.bfloat16)
    copies = jnp.broadcast_to(piece[None], (seq_size, part_rows, width))
    summed = lax.all_to_all(
        copies.reshape(seq_size * part_rows, width), "seq", split_axis=0, concat_axis=0, tiled=True
    )[:panel]
    grad_weight = summed[:, :pixel_width]
    grad_channels = summed[:, pixel_width:].astype(jnp.float32).T
    return (features[None], grad_rows[None], grad_weight, grad_channels)


def solution(mesh):
    in_specs = (
        P("fsdp", "seq", None),
        P("fsdp", "seq"),
        P("fsdp", None),
        P("fsdp", None),
        P("fsdp"),
        P(None, "fsdp"),
        P("fsdp", "seq", None),
    )
    out_specs = (P("fsdp", "seq", None), P("fsdp", "seq", None), P("fsdp", None), P(None, "fsdp"))
    return jax.shard_map(shards, mesh=mesh, in_specs=in_specs, out_specs=out_specs, check_vma=False)
```
